32 devices in a mesh: pb: 4 (over y, x), ka: 8 (over z, core).
Axes of the slice: x: 2, y: 2, z: 4, core: 2. Of those that a mesh axis runs over, the one named last changes fastest.
Arguments:
- queries: bfloat16 [4096, 512], P('pb'), may hold values from -100 to 100
- keys: bfloat16 [4096, 512], P('ka'), may hold values from -100 to 100
- values: bfloat16 [4096, 512], P('ka'), may hold values from -6 to 6
Outputs:
- attended: bfloat16 [4096, 512], P(('pb', 'ka'))
The draws below stay inside these ranges and needn't reach their ends.
All inputs are finite; a program needn't handle non-finite values.
Results may differ from the reference program's by a relative error of at most 0.005.
Values sent between devices are 32-bit elements; how exact they have to be, the bound alone decides.
No kernel may reach another device: no remote copies, remote signals or barrier semaphores. Data moves between devices by JAX's collectives and lax.ppermute only.
A program may use at most 64 MiB of HBM per device.

```python
import math
import jax
import jax.numpy as jnp
from jax import lax

H = 4
DH = 128
ITERS = 3
SEQ = 4096


def drawn_pair(key):
    base = jax.random.fold_in(key, 11)
    query_key, field_key = jax.random.split(base, 2)
    features = H * DH
    query_field = 1.7 * jax.random.truncated_normal(query_key, -5.0, 5.0, (SEQ, features), jnp.float32)
    key_field = 1.7 * jax.random.truncated_normal(field_key, -5.0, 5.0, (SEQ, features), jnp.float32)
    return (query_field, key_field)


def draw_queries(key, part):
    return drawn_pair(key)[0].astype(jnp.bfloat16)


def draw_keys(key, part):
    return drawn_pair(key)[1].astype(jnp.bfloat16)


def level_of(key, extent, cuts, low, high):
    gain = 1.0
    for dim, parts in cuts:
        steps = jax.random.uniform(jax.random.fold_in(jax.random.fold_in(key, 6), dim), (parts,), jnp.float32, low / len(cuts), high / len(cuts))
        gain = gain * jnp.repeat(jnp.exp(steps), extent[dim] // parts).reshape((-1,) + (1,) * (len(extent) - 1 - dim))
    return gain


def bell_draw(stream_key, dims, spread, most, pieces=(), held_as=jnp.bfloat16):
    factor_of = level_of(stream_key, dims, pieces, -0.22, 0.18) if pieces else 1.0
    entries = jax.random.normal(stream_key, dims, jnp.float32) * spread * factor_of
    return jnp.minimum(jnp.maximum(entries, -most), most).astype(held_as)


def setup_inputs(seed: int = 0) -> dict:
    seeds = jax.random.split(jax.random.key(seed), 4)
    return {
        "queries": draw_queries(jax.random.fold_in(seeds[3], 71), 0),
        "keys": draw_keys(jax.random.fold_in(seeds[3], 71), 0),
        "values": bell_draw(seeds[2], (SEQ, H * DH), 1.0, 6.0, ((0, 8),)),
    }


def reference(queries, keys, values):
    factor = 1.0 / math.sqrt(DH)
    head_queries = queries.reshape(SEQ, H, DH).transpose(1, 0, 2)
    head_keys = keys.reshape(SEQ, H, DH).transpose(1, 0, 2)
    head_values = values.reshape(SEQ, H, DH).transpose(1, 0, 2)

    def one_head(operands):
        query_part, key_part, value_part = operands
        scores = jnp.dot(query_part, key_part.T, preferred_element_type=jnp.float32) * factor
        row_pot = jnp.zeros((SEQ,), jnp.float32)
        col_pot = jnp.zeros((SEQ,), jnp.float32)
        for step in range(ITERS):
            col_pot = jax.nn.logsumexp(scores - row_pot[:, None], axis=0)
            row_pot = jax.nn.logsumexp(scores - col_pot[None, :], axis=1)
        weights = jnp.exp(scores - row_pot[:, None] - col_pot[None, :]).astype(jnp.bfloat16)
        return jnp.dot(weights, value_part, preferred_element_type=jnp.float32).astype(jnp.bfloat16)
    result = lax.map(one_head, (head_queries, head_keys, head_values))
    return result.transpose(1, 0, 2).reshape(SEQ, H * DH)
```

```python
import functools
import math

import jax
import jax.numpy as jnp
from jax import lax
from jax.experimental import pallas as pl
from jax.experimental.pallas import tpu as pltpu
from jax.sharding import PartitionSpec as P

H = 4
DH = 128
ITERS = 3
LANE = 128
CORES = 2
SCALE2 = math.log2(math.e) / math.sqrt(DH)
LOW, HIGH = 1e-13, 1e13
VMEM_BUDGET = 36 * 2**20
F32, BF16 = jnp.float32, jnp.bfloat16
NT = (((1,), (1,)), ((), ()))


def merged(part, axis, combine):
    gathered = jax.tree.map(lambda a: lax.all_gather(a, axis), part)

    def take(source):
        return jax.tree.map(lambda a: lax.dynamic_index_in_dim(a, source, 0, False), gathered)

    return lax.fori_loop(
        1, lax.axis_size(axis), lambda source, state: combine(state, take(source)), take(0)
    )


def merge_stats(first, second):
    peak = jnp.maximum(first[0], second[0])
    total = first[1] * jnp.exp(first[0] - peak) + second[1] * jnp.exp(second[0] - peak)
    return (peak, total)


def merged_log(peak, total, axis):
    global_peak, whole = merged((peak, total), axis, merge_stats)
    return global_peak + jnp.log(whole)


def general_body(queries, keys, values):
    q_count = queries.shape[0]
    k_count = keys.shape[0]
    factor = 1.0 / math.sqrt(DH)
    head_queries = queries.reshape(q_count, H, DH).transpose(1, 0, 2)
    head_keys = keys.reshape(k_count, H, DH).transpose(1, 0, 2)
    head_values = values.reshape(k_count, H, DH).transpose(1, 0, 2)

    def head_scores(query_part, index):
        dots = lax.dot_general(query_part, head_keys[index], NT, preferred_element_type=F32)
        return dots * factor

    row_pot = jnp.zeros((H, q_count), F32)
    col_pot = jnp.zeros((H, k_count), F32)
    for step in range(ITERS):
        peaks = []
        totals = []
        for index in range(H):
            shifted = head_scores(head_queries[index], index) - row_pot[index][:, None]
            peak = jnp.max(shifted, axis=0)
            peaks.append(peak)
            totals.append(jnp.sum(jnp.exp(shifted - peak[None, :]), axis=0))
        col_pot = merged_log(jnp.stack(peaks), jnp.stack(totals), "pb")
        peaks = []
        totals = []
        for index in range(H):
            shifted = head_scores(head_queries[index], index) - col_pot[index][None, :]
            peak = jnp.max(shifted, axis=1)
            peaks.append(peak)
            totals.append(jnp.sum(jnp.exp(shifted - peak[:, None]), axis=1))
        row_pot = merged_log(jnp.stack(peaks), jnp.stack(totals), "ka")
    pieces = []
    for index in range(H):
        scores = head_scores(head_queries[index], index)
        shifted = scores - row_pot[index][:, None] - col_pot[index][None, :]
        weights = jnp.exp(shifted).astype(BF16)
        pieces.append(jnp.dot(weights, head_values[index], preferred_element_type=F32))
    partial_sum = jnp.concatenate(pieces, axis=1)
    summed = lax.psum_scatter(partial_sum, "ka", scatter_dimension=0, tiled=True)
    return summed.astype(BF16)


def to_col(row):
    return jnp.broadcast_to(row, (LANE, LANE)).T


def to_row(col):
    return jnp.broadcast_to(col, (LANE, LANE)).T[0:1]


def in_range(x):
    return (x >= LOW) & (x <= HIGH)


def all_true(mask):
    return jnp.min(jnp.where(mask, 1.0, 0.0)) > 0.5


def split2(x):
    high = x.astype(BF16).astype(F32)
    rows = lax.broadcasted_iota(jnp.int32, (8, x.shape[1]), 0)
    both = jnp.where(rows == 0, high, jnp.where(rows == 1, x - high, 0.0))
    return both.astype(BF16)


def vec_mat(x, mat):
    out = jnp.dot(split2(x), mat, preferred_element_type=F32)
    return out[0:1] + out[1:2]


def inverse(x):
    return jnp.where(in_range(x), 1.0 / x, jnp.nan)


def scores2(q, k):
    return lax.dot_general(q, k, NT, preferred_element_type=F32) * SCALE2


def slow_cols(r_ref, q_ref, k_refs, c_ref):
    rows = q_ref.shape[0]
    for j, k_ref in enumerate(k_refs):
        count = k_ref.shape[0]
        kb = k_ref[...].astype(BF16)

        def block(b, state):
            m, l = state
            at = pl.multiple_of(b * LANE, LANE)
            s = scores2(q_ref[pl.ds(at, LANE), :], kb) - to_col(r_ref[:, pl.ds(at, LANE)])[:, 0:1]
            top = jnp.maximum(m, jnp.max(s, axis=0, keepdims=True))
            l = l * jnp.exp2(m - top) + jnp.sum(jnp.exp2(s - top), axis=0, keepdims=True)
            return top, l

        start = (jnp.full((1, count), -3e38, F32), jnp.zeros((1, count), F32))
        m, l = lax.fori_loop(0, rows // LANE, block, start)
        c_ref[:, j * count : (j + 1) * count] = m + jnp.log2(l)


def slow_block(q, k_refs, c_ref, v_refs=()):
    m = jnp.full((LANE, 1), -3e38, F32)
    l = jnp.zeros((LANE, 1), F32)
    acc = jnp.zeros((LANE, DH), F32)
    for j, k_ref in enumerate(k_refs):
        count = k_ref.shape[0]
        s = scores2(q, k_ref[...].astype(BF16)) - c_ref[:, j * count : (j + 1) * count]
        top = jnp.maximum(m, jnp.max(s, axis=1, keepdims=True))
        e = jnp.exp2(s - top)
        old = jnp.exp2(m - top)
        l = l * old + jnp.sum(e, axis=1, keepdims=True)
        if v_refs:
            v = v_refs[j][...].astype(BF16)
            acc = acc * old + jnp.dot(e.astype(BF16), v, preferred_element_type=F32)
        m = top
    return m, l, acc


def slow_rows(q_ref, k_refs, c_ref, out_ref):
    def block(b, carry):
        at = pl.multiple_of(b * LANE, LANE)
        m, l, _ = slow_block(q_ref[pl.ds(at, LANE), :], k_refs, c_ref)
        out_ref[0:1, pl.ds(at, LANE)] = to_row(l)
        out_ref[1:2, pl.ds(at, LANE)] = to_row(m)
        return carry

    lax.fori_loop(0, q_ref.shape[0] // LANE, block, 0)


def merge_rows(mine_ref, other_ref):
    t1, p1 = mine_ref[0:1, :], mine_ref[1:2, :]
    t2, p2 = other_ref[0:1, :], other_ref[1:2, :]
    peak = jnp.maximum(p1, p2)
    total = t1 * jnp.exp2(p1 - peak) + t2 * jnp.exp2(p2 - peak)
    plain = in_range(total) & (peak == 0.0) & (p1 == p2)
    return jnp.where(plain, total, jnp.nan), peak + jnp.log2(total)


def place_kernel(halves, core_ref, own_ref, mine_ref, other_ref, q_ref):
    rows = own_ref.shape[0]
    half = rows // halves
    core = core_ref[0]
    q_ref[0:rows, :] = own_ref[...]
    for k in range(mine_ref.shape[0]):
        at = (k + 1) * rows
        here = pl.multiple_of(at + core * half, half)
        there = pl.multiple_of(at + (1 - core) * half, half)
        q_ref[pl.ds(here, half), :] = mine_ref[k].astype(BF16)
        q_ref[pl.ds(there, half), :] = other_ref[k].astype(BF16)


def first_kernel(last, *refs):
    if last:
        q_ref, prev_ref, *k_refs = refs[:-5]
        e_ref, t_ref, sums_ref, r_ref, c_ref = refs[-5:]
    else:
        q_ref, prev_ref, *k_refs = refs[:-3]
        e_ref, t_ref, sums_ref = refs[-3:]
    kb = k_refs[-1][...].astype(BF16)
    rows, count = e_ref.shape
    step = 256
    cols = jnp.zeros((8, count), F32)
    for at in range(0, rows, step):
        q = q_ref[at : at + step, :]
        e = jnp.exp2(scores2(q, kb))
        e_ref[at : at + step, :] = e.astype(BF16)
        cols = cols + jnp.sum(e.reshape(step // 8, 8, count), axis=0)
        t_ref[:, at : at + step] = jnp.exp2(scores2(kb, q)).astype(BF16)
    v = inverse(jnp.sum(cols, axis=0, keepdims=True))
    total = prev_ref[0:1, :] + vec_mat(v, t_ref[...])
    sums_ref[0:1, :] = total
    sums_ref[1:2, :] = jnp.zeros_like(total)
    if last:

        @pl.when(jnp.logical_not(all_true(in_range(total))))
        def _():
            r_ref[...] = jnp.zeros_like(r_ref)
            slow_cols(r_ref, q_ref, k_refs, c_ref)
            slow_rows(q_ref, k_refs, c_ref, sums_ref)


def next_kernel(blocks, *refs):
    mine_ref, other_ref, q_ref = refs[:3]
    k_refs = refs[3 : 3 + blocks]
    e_refs = refs[3 + blocks : 3 + 2 * blocks]
    t_refs = refs[3 + 2 * blocks : 3 + 3 * blocks]
    sums_ref, r_ref, c_ref = refs[3 + 3 * blocks :]
    total, log_total = merge_rows(mine_ref, other_ref)
    u = 1.0 / total
    sums = jnp.zeros_like(total)
    for e_ref, t_ref in zip(e_refs, t_refs):
        v = inverse(vec_mat(u, e_ref[...]))
        sums = sums + vec_mat(v, t_ref[...])
    sums_ref[0:1, :] = sums
    sums_ref[1:2, :] = jnp.zeros_like(sums)
    r_ref[...] = log_total

    @pl.when(jnp.logical_not(all_true(in_range(sums))))
    def _():
        slow_cols(r_ref, q_ref, k_refs, c_ref)
        slow_rows(q_ref, k_refs, c_ref, sums_ref)


def last_kernel(blocks, heads, *refs):
    place_ref, mine_ref, other_ref, q_ref = refs[:4]
    k_refs = refs[4 : 4 + blocks]
    e_refs = refs[4 + blocks : 4 + 2 * blocks]
    v_refs = refs[4 + 2 * blocks : 4 + 3 * blocks]
    keep_ref, send_ref, r_ref, c_ref, acc_ref = refs[4 + 3 * blocks :]
    core, chip = place_ref[0], place_ref[1]
    rows = q_ref.shape[0] // heads
    owned = keep_ref.shape[0] // heads
    span = CORES * owned
    total, log_total = merge_rows(mine_ref, other_ref)
    u = 1.0 / total
    starts = [pl.multiple_of(h * rows + chip * span, span) for h in range(heads)]
    acc = jnp.zeros(acc_ref.shape, F32)
    for e_ref, v_ref in zip(e_refs, v_refs):
        v = inverse(vec_mat(u, e_ref[...]))
        count = v.shape[1]
        col = jnp.concatenate([to_col(v[:, at : at + LANE]) for at in range(0, count, LANE)], axis=0)
        high = col.astype(BF16).astype(F32)
        lanes = lax.broadcasted_iota(jnp.int32, col.shape, 1)
        both = jnp.where(lanes % 2 == 0, high, col - high)
        right = jnp.concatenate([(col * v_ref[...]).astype(BF16), both.astype(BF16)], axis=1)
        left = jnp.concatenate([e_ref[pl.ds(at, span), :] for at in starts], axis=0)
        acc = acc + jnp.dot(left, right, preferred_element_type=F32)
    stat = acc[:, DH:]
    stat = stat + pltpu.roll(stat, 1, 1)
    lanes = lax.broadcasted_iota(jnp.int32, stat.shape, 1)
    acc_ref[:, :DH] = acc[:, :DH]
    acc_ref[:, DH:] = jnp.where(lanes < LANE // 2, stat, 0.0)
    r_ref[...] = log_total

    @pl.when(jnp.logical_not(all_true(in_range(stat))))
    def _():
        slow_cols(r_ref, q_ref, k_refs, c_ref)

        def block(b, carry):
            at = pl.multiple_of((b // CORES) * rows + chip * span + (b % CORES) * owned, LANE)
            m, l, num = slow_block(q_ref[pl.ds(at, LANE), :], k_refs, c_ref, v_refs)
            to = pl.multiple_of(b * LANE, LANE)
            acc_ref[pl.ds(to, LANE), :DH] = num
            lanes = lax.broadcasted_iota(jnp.int32, (LANE, LANE), 1)
            acc_ref[pl.ds(to, LANE), DH:] = jnp.where(lanes < LANE // 2, l, m)
            return carry

        lax.fori_loop(0, acc_ref.shape[0] // LANE, block, 0)

    for h in range(heads):
        here = pl.multiple_of(h * span + core * owned, owned)
        there = pl.multiple_of(h * span + (1 - core) * owned, owned)
        keep_ref[h * owned : (h + 1) * owned, :] = acc_ref[pl.ds(here, owned), :]
        send_ref[h * owned : (h + 1) * owned, :] = acc_ref[pl.ds(there, owned), :]


def norm_kernel(mine_ref, other_ref, *out_refs):
    half = DH + LANE // 2
    t1, p1 = mine_ref[:, DH : DH + 1], mine_ref[:, half : half + 1]
    t2, p2 = other_ref[:, DH : DH + 1], other_ref[:, half : half + 1]
    peak = jnp.maximum(p1, p2)
    w1, w2 = jnp.exp2(p1 - peak), jnp.exp2(p2 - peak)
    scale = 1.0 / (t1 * w1 + t2 * w2)
    out = mine_ref[:, :DH] * (w1 * scale) + other_ref[:, :DH] * (w2 * scale)
    owned = out_refs[0].shape[0]
    for h, out_ref in enumerate(out_refs):
        out_ref[...] = out[h * owned : (h + 1) * owned, :]


def join_kernel(place_ref, *refs):
    out_ref = refs[-1]
    for k, ref in enumerate(refs[:-1]):
        at = pl.multiple_of((place_ref[2] ^ k) * DH, DH)
        out_ref[:, pl.ds(at, DH)] = ref[...].astype(BF16)


IN_VMEM = pl.BlockSpec(memory_space=pltpu.VMEM)
IN_SMEM = pl.BlockSpec(memory_space=pltpu.SMEM)


def launch(kernel, outs, args, scalars=0, scratch=(), limit=20, flops=0, transcendentals=0):
    outs = tuple(jax.ShapeDtypeStruct(shape, dtype) for shape, dtype in outs)
    moved = sum(a.size * a.dtype.itemsize for a in args) + sum(
        math.prod(o.shape) * o.dtype.itemsize for o in outs
    )
    return pl.pallas_call(
        kernel,
        out_shape=outs,
        in_specs=[IN_SMEM] * scalars + [IN_VMEM] * (len(args) - scalars),
        out_specs=tuple(IN_VMEM for _ in outs),
        scratch_shapes=scratch,
        compiler_params=pltpu.CompilerParams(vmem_limit_bytes=limit * 2**20),
        cost_estimate=pl.CostEstimate(
            flops=flops, bytes_accessed=moved, transcendentals=transcendentals
        ),
    )(*args)


def head_body(queries, keys, values):
    heads = lax.axis_size("pb")
    chips = lax.axis_size("ka") // CORES
    p = lax.axis_index("pb")
    a = lax.axis_index("ka")
    core, chip = a % CORES, a // CORES
    place = jnp.stack([core, chip, p]).astype(jnp.int32)
    q_rows, k_rows = queries.shape[0], keys.shape[0]
    rows = q_rows * heads
    half = q_rows // CORES
    owned = q_rows // (chips * CORES)

    def swap(x, axis, mask):
        size = lax.axis_size(axis)
        return lax.ppermute(x, axis, [(i, i ^ mask) for i in range(size)])

    def gather_chips(x):
        return [x] + [swap(x, "ka", CORES * k) for k in range(1, chips)]

    mine = []
    for k in range(1, heads):
        part = lax.dynamic_slice(queries, (core * half, (p ^ k) * DH), (half, DH))
        mine.append(swap(part.astype(F32), "pb", k))
    k_blocks = gather_chips(lax.dynamic_slice_in_dim(keys, p * DH, DH, 1).astype(F32))
    mine = jnp.stack(mine)
    other = swap(mine, "ka", 1)
    own = lax.dynamic_slice_in_dim(queries, p * DH, DH, 1)
    (q,) = launch(
        functools.partial(place_kernel, CORES),
        [((rows, DH), BF16)],
        [place, own, mine, other],
        scalars=1,
    )
    v_blocks = gather_chips(lax.dynamic_slice_in_dim(values, p * DH, DH, 1).astype(F32))

    work = [pltpu.VMEM((1, rows), F32), pltpu.VMEM((1, chips * k_rows), F32)]
    sums = jnp.zeros((2, rows), F32)
    e_blocks, t_blocks = [], []
    for j in range(chips):
        last = j == chips - 1
        e, t, sums = launch(
            functools.partial(first_kernel, last),
            [((rows, k_rows), BF16), ((k_rows, rows), BF16), ((2, rows), F32)],
            [q, sums, *(k_blocks if last else k_blocks[j : j + 1])],
            scratch=work if last else (),
            flops=4 * rows * k_rows * DH,
            transcendentals=2 * rows * k_rows,
        )
        e_blocks.append(e)
        t_blocks.append(t)
    for step in range(1, ITERS - 1):
        (sums,) = launch(
            functools.partial(next_kernel, chips),
            [((2, rows), F32)],
            [sums, swap(sums, "ka", 1), q, *k_blocks, *e_blocks, *t_blocks],
            scratch=work,
            flops=64 * rows * chips * k_rows,
        )
    stats = (heads * owned, DH + LANE)
    keep, send = launch(
        functools.partial(last_kernel, chips, heads),
        [(stats, F32), (stats, F32)],
        [place, sums, swap(sums, "ka", 1), q, *k_blocks, *e_blocks, *v_blocks],
        scalars=1,
        scratch=[*work, pltpu.VMEM((CORES * stats[0], stats[1]), F32)],
        flops=64 * rows * chips * k_rows,
    )
    parts = launch(norm_kernel, [((owned, DH), F32)] * heads, [keep, swap(send, "ka", 1)])
    parts = [parts[0]] + [swap(parts[k], "pb", k) for k in range(1, heads)]
    (out,) = launch(join_kernel, [((owned, heads * DH), BF16)], [place, *parts], scalars=1)
    return out


def solution(mesh):
    pb, ka = mesh.shape["pb"], mesh.shape["ka"]

    def body(queries, keys, values):
        rows = pb * queries.shape[0]
        held = 2 * 2 * rows * (ka // CORES) * keys.shape[0]
        powers = pb & (pb - 1) == 0 and ka & (ka - 1) == 0 and ka >= 2 * CORES
        if powers and pb == H and held <= VMEM_BUDGET:
            return head_body(queries, keys, values)
        return general_body(queries, keys, values)

    in_specs = (P("pb", None), P("ka", None), P("ka", None))
    out_specs = P(("pb", "ka"), None)
    return jax.shard_map(body, mesh=mesh, in_specs=in_specs, out_specs=out_specs, check_vma=False)
```

```python
import math

import jax
import jax.numpy as jnp
from jax import lax
from jax.experimental import pallas as pl
from jax.experimental.pallas import tpu as pltpu
from jax.sharding import PartitionSpec as P


H = 4
DH = 128
ITERS = 3
LANE = 128
CORES = 2
SCALE2 = math.log2(math.e) / math.sqrt(DH)
LOW, HIGH = 1e-13, 1e13
VMEM_BUDGET = 36 * 2**20
F32, BF16 = jnp.float32, jnp.bfloat16
NT = (((1,), (1,)), ((), ()))


def merged(part, axis, combine):
    gathered = jax.tree.map(lambda a: lax.all_gather(a, axis), part)

    def take(source):
        return jax.tree.map(lambda a: lax.dynamic_index_in_dim(a, source, 0, False), gathered)

    return lax.fori_loop(
        1, lax.axis_size(axis), lambda source, state: combine(state, take(source)), take(0)
    )


def merge_stats(first, second):
    peak = jnp.maximum(first[0], second[0])
    total = first[1] * jnp.exp(first[0] - peak) + second[1] * jnp.exp(second[0] - peak)
    return (peak, total)


def merged_log(peak, total, axis):
    global_peak, whole = merged((peak, total), axis, merge_stats)
    return global_peak + jnp.log(whole)


def general_body(queries, keys, values):
    q_count = queries.shape[0]
    k_count = keys.shape[0]
    factor = 1.0 / math.sqrt(DH)
    head_queries = queries.reshape(q_count, H, DH).transpose(1, 0, 2)
    head_keys = keys.reshape(k_count, H, DH).transpose(1, 0, 2)
    head_values = values.reshape(k_count, H, DH).transpose(1, 0, 2)

    def head_scores(query_part, index):
        dots = lax.dot_general(query_part, head_keys[index], NT, preferred_element_type=F32)
        return dots * factor

    row_pot = jnp.zeros((H, q_count), F32)
    col_pot = jnp.zeros((H, k_count), F32)
    for _ in range(ITERS):
        peaks = []
        totals = []
        for index in range(H):
            shifted = head_scores(head_queries[index], index) - row_pot[index][:, None]
            peak = jnp.max(shifted, axis=0)
            peaks.append(peak)
            totals.append(jnp.sum(jnp.exp(shifted - peak[None, :]), axis=0))
        col_pot = merged_log(jnp.stack(peaks), jnp.stack(totals), "pb")
        peaks = []
        totals = []
        for index in range(H):
            shifted = head_scores(head_queries[index], index) - col_pot[index][None, :]
            peak = jnp.max(shifted, axis=1)
            peaks.append(peak)
            totals.append(jnp.sum(jnp.exp(shifted - peak[:, None]), axis=1))
        row_pot = merged_log(jnp.stack(peaks), jnp.stack(totals), "ka")
    pieces = []
    for index in range(H):
        scores = head_scores(head_queries[index], index)
        shifted = scores - row_pot[index][:, None] - col_pot[index][None, :]
        weights = jnp.exp(shifted).astype(BF16)
        pieces.append(jnp.dot(weights, head_values[index], preferred_element_type=F32))
    partial_sum = jnp.concatenate(pieces, axis=1)
    summed = lax.psum_scatter(partial_sum, "ka", scatter_dimension=0, tiled=True)
    return summed.astype(BF16)


def to_col(row):
    return jnp.broadcast_to(row, (LANE, LANE)).T


def to_row(col):
    return jnp.broadcast_to(col, (LANE, LANE)).T[0:1]


def in_range(x):
    return (x >= LOW) & (x <= HIGH)


def all_true(mask):
    return jnp.min(jnp.where(mask, 1.0, 0.0)) > 0.5


def split2(x):
    high = x.astype(BF16).astype(F32)
    rows = lax.broadcasted_iota(jnp.int32, (8, x.shape[1]), 0)
    both = jnp.where(rows == 0, high, jnp.where(rows == 1, x - high, 0.0))
    return both.astype(BF16)


def inverse(x):
    return jnp.where(in_range(x), 1.0 / x, jnp.nan)


def scores2(q, k):
    return lax.dot_general(q, k, NT, preferred_element_type=F32) * SCALE2


def slow_cols(r_ref, q_refs, k_ref, count, c_ref):
    for begin in range(0, k_ref.shape[0], count):
        kb = k_ref[begin : begin + count, :]
        state = (jnp.full((1, count), -3e38, F32), jnp.zeros((1, count), F32))
        first = 0
        for q_ref in q_refs:

            def block(b, state, q_ref=q_ref, first=first):
                m, l = state
                at = pl.multiple_of(b * LANE, LANE)
                r = to_col(r_ref[:, pl.ds(first + at, LANE)])[:, 0:1]
                s = scores2(q_ref[pl.ds(at, LANE), :], kb) - r
                top = jnp.maximum(m, jnp.max(s, axis=0, keepdims=True))
                l = l * jnp.exp2(m - top) + jnp.sum(jnp.exp2(s - top), axis=0, keepdims=True)
                return top, l

            state = lax.fori_loop(0, q_ref.shape[0] // LANE, block, state)
            first += q_ref.shape[0]
        c_ref[:, begin : begin + count] = state[0] + jnp.log2(state[1])


def slow_block(q, k_ref, count, c_ref, v_ref=None):
    m = jnp.full((LANE, 1), -3e38, F32)
    l = jnp.zeros((LANE, 1), F32)
    acc = jnp.zeros((LANE, DH), F32)
    for begin in range(0, k_ref.shape[0], count):
        s = scores2(q, k_ref[begin : begin + count, :]) - c_ref[:, begin : begin + count]
        top = jnp.maximum(m, jnp.max(s, axis=1, keepdims=True))
        e = jnp.exp2(s - top)
        old = jnp.exp2(m - top)
        l = l * old + jnp.sum(e, axis=1, keepdims=True)
        if v_ref is not None:
            v = v_ref[begin : begin + count, :]
            acc = acc * old + jnp.dot(e.astype(BF16), v, preferred_element_type=F32)
        m = top
    return m, l, acc


def slow_rows(q_refs, k_ref, count, c_ref, out_ref):
    first = 0
    for q_ref in q_refs:

        def block(b, carry, q_ref=q_ref, first=first):
            at = pl.multiple_of(b * LANE, LANE)
            m, l, _ = slow_block(q_ref[pl.ds(at, LANE), :], k_ref, count, c_ref)
            out_ref[0:1, pl.ds(first + at, LANE)] = to_row(l)
            out_ref[1:2, pl.ds(first + at, LANE)] = to_row(m)
            return carry

        lax.fori_loop(0, q_ref.shape[0] // LANE, block, 0)
        first += q_ref.shape[0]


def merge_rows(mine_ref, other_ref):
    t1, p1 = mine_ref[0:1, :], mine_ref[1:2, :]
    t2, p2 = other_ref[0:1, :], other_ref[1:2, :]
    peak = jnp.maximum(p1, p2)
    total = t1 * jnp.exp2(p1 - peak) + t2 * jnp.exp2(p2 - peak)
    plain = in_range(total) & (peak == 0.0) & (p1 == p2)
    return jnp.where(plain, total, jnp.nan), peak + jnp.log2(total)


def added(refs):
    out = refs[0][...]
    for ref in refs[1:]:
        out = out + ref[...]
    return out


def place(place_ref, mine_ref, other_ref, q_ref):
    blocks, half, _ = mine_ref.shape
    core = place_ref[0]
    for k in range(blocks):
        here = pl.multiple_of((CORES * k + core) * half, half)
        there = pl.multiple_of((CORES * k + 1 - core) * half, half)
        q_ref[pl.ds(here, half), :] = mine_ref[k].astype(BF16)
        q_ref[pl.ds(there, half), :] = other_ref[k].astype(BF16)


def exponents(q_ref, kb, e_ref, t_ref, cols_ref):
    rows, count = e_ref.shape
    step = min(256, rows)
    cols = jnp.zeros((8, count), F32)
    for at in range(0, rows, step):
        q = q_ref[at : at + step, :]
        e = jnp.exp2(scores2(q, kb))
        cols = cols + jnp.sum(e.reshape(step // 8, 8, count), axis=0)
        e = e.astype(BF16)
        e_ref[at : at + step, :] = e
        t_ref[:, at : at + step] = e.T
    cols_ref[...] = jnp.sum(cols, axis=0, keepdims=True)


def add_rows(sums_ref, v, t_refs, begin):
    v = split2(v)
    at = 0
    for t_ref in t_refs:
        out = jnp.dot(v, t_ref[...], preferred_element_type=F32)
        out = out[0:1] + out[1:2]
        to = slice(at, at + t_ref.shape[1])
        sums_ref[0:1, to] = out if begin else sums_ref[0:1, to] + out
        at += t_ref.shape[1]


def col_sums(u, e_refs):
    at, total = 0, 0.0
    for e_ref in e_refs:
        total = total + jnp.dot(u[:, at : at + e_ref.shape[0]], e_ref[...], preferred_element_type=F32)
        at += e_ref.shape[0]
    return total[0:1] + total[1:2]


def make_kernel(q_refs, k_refs, outs):
    for j, k_parts in enumerate(k_refs):
        kb = added(k_parts).astype(BF16)
        for g, q_ref in enumerate(q_refs):
            exponents(q_ref, kb, *outs[g][j])


def place_kernel(place_ref, mine_ref, other_ref, k_refs, q_ref, outs):
    place(place_ref, mine_ref, other_ref, q_ref)
    make_kernel([q_ref], k_refs, outs)


def early_kernel(place_ref, mine_ref, other_ref, k_refs, t_old, cols_old, q_ref, outs, sums_ref):
    place(place_ref, mine_ref, other_ref, q_ref)
    make_kernel([q_ref], k_refs, outs)
    for j in range(len(k_refs)):
        _, t_ref, cols_ref = outs[0][j]
        total = cols_ref[...]
        for old_ref in cols_old[j]:
            total = total + old_ref[...]
        add_rows(sums_ref, inverse(total), [*t_old[j], t_ref], j == 0)


def late_kernel(q_refs, k_refs, prev_ref, outs, sums_ref, all_ref, r_ref, c_ref):
    count = k_refs[-1][0].shape[0]
    for j, k_parts in enumerate(k_refs):
        all_ref[j * count : (j + 1) * count, :] = added(k_parts).astype(BF16)
    kb = all_ref[all_ref.shape[0] - count :, :]
    total = 0.0
    for g, q_ref in enumerate(q_refs):
        exponents(q_ref, kb, *outs[g][0])
        total = total + outs[g][0][2][...]
    sums_ref[0:1, :] = prev_ref[...]
    sums_ref[1:2, :] = jnp.zeros_like(prev_ref)
    add_rows(sums_ref, inverse(total), [outs[g][0][1] for g in range(len(q_refs))], False)

    @pl.when(jnp.logical_not(all_true(in_range(sums_ref[0:1, :]))))
    def _():
        r_ref[...] = jnp.zeros_like(r_ref)
        slow_cols(r_ref, q_refs, all_ref, count, c_ref)
        slow_rows(q_refs, all_ref, count, c_ref, sums_ref)


def next_kernel(mine_ref, other_ref, q_refs, all_ref, e_refs, t_refs, sums_ref, r_ref, c_ref):
    total, log_total = merge_rows(mine_ref, other_ref)
    u = split2(1.0 / total)
    for j in range(len(e_refs)):
        add_rows(sums_ref, inverse(col_sums(u, e_refs[j])), t_refs[j], j == 0)
    sums_ref[1:2, :] = jnp.zeros_like(total)
    r_ref[...] = log_total

    @pl.when(jnp.logical_not(all_true(in_range(sums_ref[0:1, :]))))
    def _():
        count = e_refs[0][0].shape[1]
        slow_cols(r_ref, q_refs, all_ref, count, c_ref)
        slow_rows(q_refs, all_ref, count, c_ref, sums_ref)


def last_kernel(
    place_ref, mine_ref, other_ref, q_refs, all_ref, e_refs, v_refs,
    keep_ref, send_ref, r_ref, c_ref, acc_ref, v_ref,
):
    core, chip = place_ref[0], place_ref[1]
    owned = keep_ref.shape[0] // H
    span = CORES * owned
    rows = q_refs[0].shape[0]
    blocks = [(g, at) for g, q_ref in enumerate(q_refs) for at in range(0, q_ref.shape[0], rows)]
    total, log_total = merge_rows(mine_ref, other_ref)
    u = split2(1.0 / total)
    acc = jnp.zeros(acc_ref.shape, F32)
    for j in range(len(e_refs)):
        v = inverse(col_sums(u, e_refs[j]))
        count = v.shape[1]
        col = jnp.concatenate([to_col(v[:, at : at + LANE]) for at in range(0, count, LANE)], axis=0)
        high = col.astype(BF16).astype(F32)
        lanes = lax.broadcasted_iota(jnp.int32, col.shape, 1)
        both = jnp.where(lanes % 2 == 0, high, col - high)
        value = added(v_refs[j])
        v_ref[j * count : (j + 1) * count, :] = value.astype(BF16)
        right = jnp.concatenate([(col * value).astype(BF16), both.astype(BF16)], axis=1)
        left = [e_refs[j][g][pl.ds(pl.multiple_of(at + chip * span, span), span), :] for g, at in blocks]
        acc = acc + jnp.dot(jnp.concatenate(left, axis=0), right, preferred_element_type=F32)
    stat = acc[:, DH:]
    stat = stat + pltpu.roll(stat, 1, 1)
    lanes = lax.broadcasted_iota(jnp.int32, stat.shape, 1)
    acc_ref[:, :DH] = acc[:, :DH]
    acc_ref[:, DH:] = jnp.where(lanes < LANE // 2, stat, 0.0)
    r_ref[...] = log_total

    @pl.when(jnp.logical_not(all_true(in_range(stat))))
    def _():
        count = e_refs[0][0].shape[1]
        slow_cols(r_ref, q_refs, all_ref, count, c_ref)
        for h, (g, begin) in enumerate(blocks):

            def block(b, carry, q_ref=q_refs[g], begin=begin, h=h):
                at = pl.multiple_of(begin + chip * span + b * LANE, LANE)
                m, l, num = slow_block(q_ref[pl.ds(at, LANE), :], all_ref, count, c_ref, v_ref)
                to = pl.multiple_of(h * span + b * LANE, LANE)
                acc_ref[pl.ds(to, LANE), :DH] = num
                lanes = lax.broadcasted_iota(jnp.int32, (LANE, LANE), 1)
                acc_ref[pl.ds(to, LANE), DH:] = jnp.where(lanes < LANE // 2, l, m)
                return carry

            lax.fori_loop(0, span // LANE, block, 0)

    for h in range(len(blocks)):
        here = pl.multiple_of(h * span + core * owned, owned)
        there = pl.multiple_of(h * span + (1 - core) * owned, owned)
        keep_ref[h * owned : (h + 1) * owned, :] = acc_ref[pl.ds(here, owned), :]
        send_ref[h * owned : (h + 1) * owned, :] = acc_ref[pl.ds(there, owned), :]


def norm_kernel(mine_ref, other_ref, out_refs):
    half = DH + LANE // 2
    t1, p1 = mine_ref[:, DH : DH + 1], mine_ref[:, half : half + 1]
    t2, p2 = other_ref[:, DH : DH + 1], other_ref[:, half : half + 1]
    peak = jnp.maximum(p1, p2)
    w1, w2 = jnp.exp2(p1 - peak), jnp.exp2(p2 - peak)
    scale = 1.0 / (t1 * w1 + t2 * w2)
    out = mine_ref[:, :DH] * (w1 * scale) + other_ref[:, :DH] * (w2 * scale)
    owned = out_refs[0].shape[0]
    for h, out_ref in enumerate(out_refs):
        out_ref[...] = out[h * owned : (h + 1) * owned, :]


def join_kernel(place_ref, refs, out_ref):
    for k, ref in enumerate(refs):
        at = pl.multiple_of((place_ref[2] ^ k) * DH, DH)
        out_ref[:, pl.ds(at, DH)] = ref[...].astype(BF16)


def shape(dims, dtype=F32):
    return jax.ShapeDtypeStruct(dims, dtype)


def launch(kernel, outs, args, scratch=(), limit=6, flops=0, transcendentals=0):
    return call(kernel, outs, args, scratch, limit, flops, transcendentals)


def call(kernel, outs, args, scratch, limit, flops, transcendentals):
    in_specs = jax.tree.map(
        lambda a: pl.BlockSpec(memory_space=pltpu.SMEM if a.dtype == jnp.int32 else pltpu.VMEM), args
    )
    out_specs = jax.tree.map(lambda o: pl.BlockSpec(memory_space=pltpu.VMEM), outs)
    moved = sum(a.size * a.dtype.itemsize for a in jax.tree.leaves((args, outs)))
    return pl.pallas_call(
        kernel,
        out_shape=outs,
        in_specs=in_specs,
        out_specs=out_specs,
        scratch_shapes=scratch,
        compiler_params=pltpu.CompilerParams(vmem_limit_bytes=limit * 2**20),
        cost_estimate=pl.CostEstimate(
            flops=flops, bytes_accessed=moved, transcendentals=transcendentals
        ),
    )(*args)


def head_body(queries, keys, values):
    chips = lax.axis_size("ka") // CORES
    p = lax.axis_index("pb")
    a = lax.axis_index("ka")
    core, chip = a % CORES, a // CORES
    where = jnp.stack([core, chip, p]).astype(jnp.int32)
    q_rows, k_rows = queries.shape[0], keys.shape[0]
    rows = q_rows * H
    half = q_rows // CORES
    owned = q_rows // (chips * CORES)

    def permute(x, axis, target):
        pairs = [(i, target(i)) for i in range(lax.axis_size(axis))]
        return lax.ppermute(x, axis, [(i, t) for i, t in pairs if t is not None])

    def swap(x, axis, mask):
        return permute(x, axis, lambda i: i ^ mask)

    def inner(i):
        return 0 < i // CORES < chips - 1

    def gather_chips(x):
        far = swap(x, "ka", 2 * CORES)
        middle = permute(x, "ka", lambda i: i ^ (3 * CORES) if inner(i) else None)
        near = swap(x, "ka", CORES)
        relay = permute(far, "ka", lambda i: i ^ CORES if inner(i) else None)
        return [[x], [far], [near], [middle, relay]]

    def head(x, h):
        return lax.dynamic_slice_in_dim(x, h * DH, DH, 1)

    def made(groups, blocks):
        return [
            [(shape((g, k_rows), BF16), shape((k_rows, g), BF16), shape((1, k_rows))) for _ in range(blocks)]
            for g in groups
        ]

    def cost(groups, blocks):
        pairs = sum(groups) * blocks * k_rows
        return dict(flops=4 * pairs * DH, transcendentals=2 * pairs)

    k_blocks = gather_chips(head(keys, p).astype(F32))

    mine = {}
    for k in (3, 1, 2):
        part = lax.dynamic_slice(queries, (core * half, (p ^ k) * DH), (half, DH))
        mine[k] = swap(part.astype(F32), "pb", k)
    mine_b, mine_c = jnp.stack([mine[1], mine[2]]), mine[3][None]
    other_b, other_c = swap(mine_b, "ka", 1), swap(mine_c, "ka", 1)
    q_a = head(queries, p)
    size_a, size_b, size_c = q_rows, 2 * q_rows, q_rows

    (out_a,) = launch(make_kernel, [made([size_a], 1)], [[q_a], k_blocks[:1]], **cost([size_a], 1))
    q_b, out_b = launch(
        place_kernel,
        [shape((size_b, DH), BF16), made([size_b], 1)],
        [where, mine_b, other_b, k_blocks[:1]],
        **cost([size_b], 1),
    )
    early = [[out_a[0][0], out_b[0][0]]]
    for j in (1, 2):
        (out,) = launch(
            make_kernel,
            [made([size_a, size_b], 1)],
            [[q_a, q_b], k_blocks[j : j + 1]],
            **cost([size_a, size_b], 1),
        )
        early.append([out[0][0], out[1][0]])
    q_c, out_c, sums = launch(
        early_kernel,
        [shape((size_c, DH), BF16), made([size_c], 3), shape((1, rows))],
        [where, mine_c, other_c, k_blocks[:3], [[o[1] for o in e] for e in early], [[o[2] for o in e] for e in early]],
        **cost([size_c], 3),
    )
    q_parts = [q_a, q_b, q_c]
    work = [pltpu.VMEM((1, rows), F32), pltpu.VMEM((1, chips * k_rows), F32)]
    out_d, sums, k_all = launch(
        late_kernel,
        [made([size_a, size_b, size_c], 1), shape((2, rows)), shape((chips * k_rows, DH), BF16)],
        [q_parts, k_blocks, sums],
        scratch=work,
        **cost([size_a, size_b, size_c], 1),
    )
    blocks = [early[j] + [out_c[0][j]] for j in range(3)] + [[o[0] for o in out_d]]
    e_blocks = [[o[0] for o in b] for b in blocks]
    t_blocks = [[o[1] for o in b] for b in blocks]

    held, _ = lax.optimization_barrier((values, k_blocks[1]))
    v_blocks = gather_chips(head(held, p).astype(F32))

    for _ in range(1, ITERS - 1):
        (sums,) = launch(
            next_kernel,
            [shape((2, rows))],
            [sums, swap(sums, "ka", 1), q_parts, k_all, e_blocks, t_blocks],
            scratch=work,
            flops=64 * rows * chips * k_rows,
        )
    stats = (H * owned, DH + LANE)
    keep, send = launch(
        last_kernel,
        [shape(stats), shape(stats)],
        [where, sums, swap(sums, "ka", 1), q_parts, k_all, e_blocks, v_blocks],
        scratch=[
            *work,
            pltpu.VMEM((CORES * stats[0], stats[1]), F32),
            pltpu.VMEM((chips * k_rows, DH), BF16),
        ],
        limit=12,
        flops=64 * rows * chips * k_rows,
    )
    (parts,) = launch(norm_kernel, [[shape((owned, DH))] * H], [keep, swap(send, "ka", 1)])
    parts = [parts[0]] + [swap(parts[k], "pb", k) for k in range(1, H)]
    (out,) = launch(join_kernel, [shape((owned, H * DH), BF16)], [where, parts])
    return out


def solution(mesh):
    pb, ka = mesh.shape["pb"], mesh.shape["ka"]

    def body(queries, keys, values):
        rows = pb * queries.shape[0]
        held = 2 * 2 * rows * (ka // CORES) * keys.shape[0]
        if pb == H and ka == 4 * CORES and held <= VMEM_BUDGET:
            return head_body(queries, keys, values)
        return general_body(queries, keys, values)

    in_specs = (P("pb", None), P("ka", None), P("ka", None))
    out_specs = P(("pb", "ka"), None)
    return jax.shard_map(body, mesh=mesh, in_specs=in_specs, out_specs=out_specs, check_vma=False)
```
